32 devices in a mesh: state: 4 (over z), basis: 8 (over y, x, core).
Axes of the slice: x: 2, y: 2, z: 4, core: 2. Of those that a mesh axis runs over, the one named last changes fastest.
Arguments:
- states: float32 [8, 64, 64000], P('state', 'basis'), may hold values from -40 to 40
- membrane_step: float32 [40, 40], replicated, may hold values from -1 to 1
- cavity_forward: float32 [64, 64], replicated, may hold values from -0.75 to 0.75
- coupling: float32 [64, 40], replicated, may hold values from 0.25 to 1
- membrane_forward: float32 [40, 40], replicated, may hold values from -1 to 1
- cavity_back: float32 [64, 64], replicated, may hold values from -9 to 9
- membrane_back: float32 [40, 40], replicated, may hold values from -1 to 1
Outputs:
- orthonormal: float32 [8, 64, 64000], P('state', 'basis')
The draws below stay inside these ranges and needn't reach their ends.
All inputs are finite; a program needn't handle non-finite values.
Results may differ from the reference program's by a relative error of at most 0.000075.
Values sent between devices are 32-bit elements; how exact they have to be, the bound alone decides.
A program may use at most 192 MiB of HBM per device.

```python
import math
import jax
import jax.numpy as jnp
from jax import lax

C = 64
M = 40
STATES = 8


def draw_states(key, part):
    key_values, key_scale = jax.random.split(key, 2)
    full_shape = (STATES, C, M * M * M)
    scales = 10.0 ** jax.random.uniform(key_scale, (STATES, 1, 1), jnp.float32)
    independent = jax.random.truncated_normal(key_values, -4.0, 4.0, full_shape, jnp.float32)
    return independent * scales


def draw_cavity_back(key, part):
    key_values, key_scale = jax.random.split(key, 2)
    levels = jnp.arange(C, dtype=jnp.float32)[:, None]
    ramped = jnp.sqrt(1.0 + 2.0 * levels / float(C - 1))
    entries = jax.random.truncated_normal(key_values, -4.0, 4.0, (C, C), jnp.float32)
    exponent = jax.random.uniform(key_scale, (C, 1), jnp.float32)
    return entries * float(C) ** (-0.5) * ramped * 10.0 ** exponent


def normal_values(stream_key, shape, spread, most, kind=jnp.bfloat16):
    return jnp.clip(spread * jax.random.normal(stream_key, shape, jnp.float32), -most, most).astype(kind)


def setup_inputs(seed: int = 0) -> dict:
    key_of = jax.random.split(jax.random.key(seed), 8)
    states = draw_states(jax.random.fold_in(key_of[7], 71), 0)
    membrane_step = normal_values(key_of[1], (M, M), M ** -0.5, 1.0, jnp.float32)
    cavity_forward = normal_values(key_of[2], (C, C), C ** -0.5, 0.75, jnp.float32)
    coupling = jnp.clip(jnp.exp(jax.random.uniform(key_of[3], (C, M), jnp.float32, math.log(0.25), math.log(1.0))), 0.25, 1.0)
    membrane_forward = normal_values(key_of[4], (M, M), M ** -0.5, 1.0, jnp.float32)
    cavity_back = draw_cavity_back(jax.random.fold_in(key_of[7], 71), 0)
    membrane_back = normal_values(key_of[6], (M, M), M ** -0.5, 1.0, jnp.float32)
    return {"states": states, "membrane_step": membrane_step, "cavity_forward": cavity_forward, "coupling": coupling, "membrane_forward": membrane_forward, "cavity_back": cavity_back, "membrane_back": membrane_back}


def propagate_state(state, membrane_step, cavity_forward, coupling, membrane_forward, cavity_back, membrane_back):
    joint = M * M * M
    highest = lax.Precision.HIGHEST
    head = jnp.einsum('ab,cbr->car', membrane_step, state.reshape(C, M, joint // M), precision=highest).reshape(C, joint)
    grid = jnp.dot(cavity_forward, head, precision=highest)
    grid = jnp.einsum('qtk,nk->qtn', grid.reshape(C, joint // M, M), membrane_forward, precision=highest)
    weighted = grid * coupling[:, None, :]
    backward = jnp.einsum('qtn,kn->qtk', weighted, membrane_back, precision=highest).reshape(C, joint)
    return jnp.dot(cavity_back, backward, precision=highest)

def reference(states, membrane_step, cavity_forward, coupling, membrane_forward, cavity_back, membrane_back):
    joint = M * M * M
    highest = lax.Precision.HIGHEST

    def single(state):
        return propagate_state(state, membrane_step, cavity_forward, coupling, membrane_forward, cavity_back, membrane_back)
    propagated = lax.map(single, states)
    flattened = propagated.reshape(STATES, C * joint)
    gram = jnp.dot(flattened, flattened.T, precision=highest) / float(C * joint)
    lower_factor = jnp.linalg.cholesky(gram)
    identity = jnp.eye(STATES, dtype=gram.dtype)
    inverse = lax.linalg.triangular_solve(lower_factor, identity, left_side=True, lower=True)
    orthonormal = jnp.dot(inverse, flattened, precision=highest)
    return orthonormal.reshape(STATES, C, joint)
```

```python
import functools

import jax
import jax.numpy as jnp
from jax import lax
from jax.experimental import pallas as pl
from jax.experimental.pallas import tpu as pltpu
from jax.sharding import PartitionSpec as P

LANES = 128
GROUP_BLOCKS = 16
VMEM_LIMIT = 60 * 1024 * 1024


def plain_body(
    states, membrane_step, cavity_forward, coupling, membrane_forward, cavity_back, membrane_back
):
    highest = lax.Precision.HIGHEST
    panel_size, level_count, joint = states.shape
    levels_all = cavity_forward.shape[0]
    membrane_levels = membrane_step.shape[0]
    basis_total = float(levels_all * joint)
    head = jnp.einsum(
        "ab,scbr->scar",
        membrane_step,
        states.reshape(panel_size, level_count, membrane_levels, joint // membrane_levels),
        precision=highest,
    )
    head = head.reshape(panel_size, level_count, joint)
    panel_block = lax.all_to_all(head, "basis", split_axis=2, concat_axis=1, tiled=True)
    items, cavity_all, columns = panel_block.shape
    grid = jnp.einsum("qc,kcr->kqr", cavity_forward, panel_block, precision=highest)
    grid = jnp.einsum(
        "kqtm,nm->kqtn",
        grid.reshape(items, cavity_all, columns // membrane_levels, membrane_levels),
        membrane_forward,
        precision=highest,
    )
    weighted = grid * coupling[None, :, None, :]
    backward = jnp.einsum("kqtn,mn->kqtm", weighted, membrane_back, precision=highest)
    backward = backward.reshape(items, cavity_all, columns)
    stepped = jnp.einsum("cq,kqr->kcr", cavity_back, backward, precision=highest)
    spread = lax.all_to_all(stepped, "state", split_axis=2, concat_axis=0, tiled=True)
    state_total, spread_levels, spread_cols = spread.shape
    flattened = spread.reshape(state_total, -1)
    partial_gram = jnp.dot(flattened, flattened.T, precision=highest)
    gram = lax.psum(partial_gram, ("state", "basis")) / basis_total
    lower_factor = jnp.linalg.cholesky(gram)
    identity = jnp.eye(state_total, dtype=gram.dtype)
    inverse = lax.linalg.triangular_solve(lower_factor, identity, left_side=True, lower=True)
    local_result = jnp.dot(inverse, flattened, precision=highest)
    local_result = local_result.reshape(state_total, spread_levels, spread_cols)
    return lax.all_to_all(
        lax.all_to_all(local_result, "state", split_axis=0, concat_axis=2, tiled=True),
        "basis",
        split_axis=1,
        concat_axis=2,
        tiled=True,
    )


def split2(x):
    hi = x.astype(jnp.bfloat16)
    lo = (x - hi.astype(jnp.float32)).astype(jnp.bfloat16)
    return hi, lo


def bdot(a, b):
    return jnp.dot(a, b, preferred_element_type=jnp.float32)


def left3(wh, wl, x):
    xh, xl = split2(x)
    return bdot(jnp.concatenate([wh, wl, wh], axis=1), jnp.concatenate([xh, xh, xl], axis=0))


def right3(x, wh, wl):
    xh, xl = split2(x)
    return bdot(xh, wh) + bdot(xl, wh) + bdot(xh, wl)


def kron_left(w, reps, out_ref_h, out_ref_l):
    m = w.shape[0]
    n = m * reps
    row = lax.broadcasted_iota(jnp.int32, (n, m), 0)
    col = lax.broadcasted_iota(jnp.int32, (n, m), 1)
    left = (row // reps == col).astype(jnp.bfloat16)
    right_row = lax.broadcasted_iota(jnp.int32, (m, n), 0)
    right_col = lax.broadcasted_iota(jnp.int32, (m, n), 1)
    right = (right_col // reps == right_row).astype(jnp.bfloat16)
    a = lax.broadcasted_iota(jnp.int32, (n, n), 0)
    b = lax.broadcasted_iota(jnp.int32, (n, n), 1)
    keep = lax.rem(a, reps) == lax.rem(b, reps)
    for part, ref in zip(split2(w), (out_ref_h, out_ref_l)):
        full = bdot(bdot(left, part).astype(jnp.bfloat16), right)
        ref[...] = jnp.where(keep, full, 0.0).astype(jnp.bfloat16)


def kron_lanes(w_t, reps, out_ref_h, out_ref_l):
    m = w_t.shape[0]
    n = m * reps
    left = (
        lax.rem(lax.broadcasted_iota(jnp.int32, (n, m), 0), m)
        == lax.broadcasted_iota(jnp.int32, (n, m), 1)
    ).astype(jnp.bfloat16)
    right = (
        lax.rem(lax.broadcasted_iota(jnp.int32, (m, n), 1), m)
        == lax.broadcasted_iota(jnp.int32, (m, n), 0)
    ).astype(jnp.bfloat16)
    a = lax.broadcasted_iota(jnp.int32, (n, n), 0)
    b = lax.broadcasted_iota(jnp.int32, (n, n), 1)
    keep = a // m == b // m
    for part, ref in zip(split2(w_t), (out_ref_h, out_ref_l)):
        full = bdot(bdot(left, part).astype(jnp.bfloat16), right)
        ref[...] = jnp.where(keep, full, 0.0).astype(jnp.bfloat16)


def head_kernel(x_ref, w_ref, o_ref, kh, kl, xs):
    nb, _, nq, lev, width = o_ref.shape
    m = w_ref.shape[0]
    cols = x_ref.shape[2] // m

    @pl.when(pl.program_id(0) == 0)
    def _():
        kron_left(w_ref[...], lev, kh, kl)
        xs[...] = jnp.zeros_like(xs)

    for i in range(m):
        xs[i * lev : (i + 1) * lev, :cols] = x_ref[0, :, i * cols : (i + 1) * cols]
    xh, xl = split2(xs[...])
    y = bdot(kh[...], xh) + bdot(kl[...], xh) + bdot(kh[...], xl)
    o_ref[...] = y.reshape(nb, 1, nq, lev, width)


def step_kernel(x_ref, fc_ref, cp_ref, fk_ref, bc_ref, bk_ref, o_ref, fh, fl, bh, bl, cps, work):
    nb, ns, _, lev, width = x_ref.shape
    c_all = fc_ref.shape[0]
    m = fk_ref.shape[0]
    group = m * GROUP_BLOCKS

    @pl.when(pl.program_id(0) == 0)
    def _():
        kron_lanes(fk_ref[...].T, GROUP_BLOCKS, fh, fl)
        kron_lanes(bk_ref[...].T, GROUP_BLOCKS, bh, bl)
        spread = (
            lax.rem(lax.broadcasted_iota(jnp.int32, (m, group), 1), m)
            == lax.broadcasted_iota(jnp.int32, (m, group), 0)
        ).astype(jnp.float32)
        cps[...] = jnp.dot(cp_ref[...], spread, precision=lax.Precision.HIGHEST)

    ch, cl = split2(fc_ref[...])
    for s in range(ns):
        x = x_ref[:, s, 0].reshape(c_all, width)
        work[s * c_all : (s + 1) * c_all, :] = left3(ch, cl, x)
    for at in range(0, width, group):
        n = min(group, width - at)
        g = right3(work[:, at : at + n], fh[:n, :n], fl[:n, :n])
        g = (g.reshape(ns, c_all, n) * cps[:, :n][None]).reshape(ns * c_all, n)
        work[:, at : at + n] = right3(g, bh[:n, :n], bl[:n, :n])
    dh, dl = split2(bc_ref[...])
    nz, half = o_ref.shape[0], o_ref.shape[1]
    for s in range(ns):
        y = left3(dh, dl, work[s * c_all : (s + 1) * c_all, :])
        o_ref[:, :, s, 0] = y.reshape(nz, half, lev, width)


def gram_kernel(x_ref, o_ref):
    nz, half, ns, nq, lev, width = x_ref.shape
    total = nz * ns
    tiles = width // LANES
    pairs = [(a, b) for a in range(total) for b in range(a + 1)]

    def outer(hq, accs):
        h, q = hq // nq, lax.rem(hq, nq)
        accs = list(accs)
        for t in range(tiles):
            vals = [
                x_ref[a // ns, h, a % ns, q, :, t * LANES : (t + 1) * LANES] for a in range(total)
            ]
            for p, (a, b) in enumerate(pairs):
                accs[p] = accs[p] + vals[a] * vals[b]
        return tuple(accs)

    zero = jnp.zeros((lev, LANES), jnp.float32)
    accs = lax.fori_loop(0, half * nq, outer, (zero,) * len(pairs))
    row = lax.broadcasted_iota(jnp.int32, (total, LANES), 0)
    col = lax.broadcasted_iota(jnp.int32, (total, LANES), 1)
    out = jnp.zeros((total, LANES), jnp.float32)
    for p, (a, b) in enumerate(pairs):
        v = jnp.sum(jnp.sum(accs[p], axis=0, keepdims=True), axis=1, keepdims=True)
        here = ((row == a) & (col == b)) | ((row == b) & (col == a))
        out = jnp.where(here, v, out)
    o_ref[...] = out


def mix_kernel(inv_ref, x_ref, o_ref):
    nz, half, ns, nq, lev, width = x_ref.shape
    total = nz * ns
    for t in range(width // LANES):
        at = slice(t * LANES, (t + 1) * LANES)
        vals = [x_ref[a // ns, 0, a % ns, 0, :, at] for a in range(total)]
        for b in range(total):
            acc = inv_ref[b, 0] * vals[0]
            for a in range(1, total):
                acc = acc + inv_ref[b, a] * vals[a]
            o_ref[b // ns, 0, b % ns, 0, :, at] = acc


def place_kernel(x_ref, o_ref):
    nb, _, nq, lev, width = x_ref.shape
    cols = o_ref.shape[2] // (nb * nq)
    for b in range(nb):
        for q in range(nq):
            i = b * nq + q
            o_ref[0, :, i * cols : (i + 1) * cols] = x_ref[b, 0, q, :, :cols]


def fast_body(
    nz,
    nb,
    states,
    membrane_step,
    cavity_forward,
    coupling,
    membrane_forward,
    cavity_back,
    membrane_back,
):
    f32 = jnp.float32
    ns, lev, joint = states.shape
    m = membrane_step.shape[0]
    c_all = cavity_forward.shape[0]
    nq, half = m // nb, nb // nz
    cols = joint // m
    width = -(-cols // LANES) * LANES
    group = m * GROUP_BLOCKS
    params = pltpu.CompilerParams(vmem_limit_bytes=VMEM_LIMIT)
    whole = lambda a: pl.BlockSpec(a.shape, lambda *_: (0,) * a.ndim)

    head = pl.pallas_call(
        head_kernel,
        grid=(ns,),
        in_specs=[pl.BlockSpec((1, lev, joint), lambda s: (s, 0, 0)), whole(membrane_step)],
        out_specs=pl.BlockSpec((nb, 1, nq, lev, width), lambda s: (0, s, 0, 0, 0)),
        out_shape=jax.ShapeDtypeStruct((nb, ns, nq, lev, width), f32),
        scratch_shapes=[
            pltpu.VMEM((m * lev, m * lev), jnp.bfloat16),
            pltpu.VMEM((m * lev, m * lev), jnp.bfloat16),
            pltpu.VMEM((m * lev, width), f32),
        ],
        compiler_params=params,
    )(states, membrane_step)
    block = lax.all_to_all(head, "basis", split_axis=0, concat_axis=0, tiled=True)
    stepped = pl.pallas_call(
        step_kernel,
        grid=(nq,),
        in_specs=[
            pl.BlockSpec((nb, ns, 1, lev, width), lambda q: (0, 0, q, 0, 0)),
            whole(cavity_forward),
            whole(coupling),
            whole(membrane_forward),
            whole(cavity_back),
            whole(membrane_back),
        ],
        out_specs=pl.BlockSpec((nz, half, ns, 1, lev, width), lambda q: (0, 0, 0, q, 0, 0)),
        out_shape=jax.ShapeDtypeStruct((nz, half, ns, nq, lev, width), f32),
        scratch_shapes=[pltpu.VMEM((group, group), jnp.bfloat16)] * 4
        + [pltpu.VMEM((c_all, group), f32), pltpu.VMEM((ns * c_all, width), f32)],
        compiler_params=params,
    )(block, cavity_forward, coupling, membrane_forward, cavity_back, membrane_back)
    spread = lax.all_to_all(stepped, "state", split_axis=0, concat_axis=0, tiled=True)
    total = nz * ns
    partial = pl.pallas_call(
        gram_kernel,
        out_shape=jax.ShapeDtypeStruct((total, LANES), f32),
        compiler_params=params,
    )(spread)
    gram = lax.psum(partial[:, :total], ("state", "basis")) / float(c_all * joint)
    lower_factor = jnp.linalg.cholesky(gram)
    identity = jnp.eye(total, dtype=f32)
    inverse = lax.linalg.triangular_solve(lower_factor, identity, left_side=True, lower=True)
    spec = pl.BlockSpec((nz, 1, ns, 1, lev, width), lambda h, q: (0, h, 0, q, 0, 0))
    mixed = pl.pallas_call(
        mix_kernel,
        grid=(half, nq),
        in_specs=[pl.BlockSpec(memory_space=pltpu.SMEM), spec],
        out_specs=spec,
        out_shape=jax.ShapeDtypeStruct(spread.shape, f32),
        compiler_params=params,
    )(inverse, spread)
    back = lax.all_to_all(mixed, "state", split_axis=0, concat_axis=0, tiled=True)
    back = back.reshape(nb, ns, nq, lev, width)
    back = lax.all_to_all(back, "basis", split_axis=0, concat_axis=0, tiled=True)
    return pl.pallas_call(
        place_kernel,
        grid=(ns,),
        in_specs=[pl.BlockSpec((nb, 1, nq, lev, width), lambda s: (0, s, 0, 0, 0))],
        out_specs=pl.BlockSpec((1, lev, joint), lambda s: (s, 0, 0)),
        out_shape=jax.ShapeDtypeStruct((ns, lev, joint), f32),
        compiler_params=params,
    )(back)


def solution(mesh):
    nz, nb = mesh.shape["state"], mesh.shape["basis"]
    in_specs = (P("state", "basis", None), P(), P(), P(), P(), P(), P())
    out_specs = P("state", "basis", None)

    def body(states, membrane_step, cavity_forward, *rest):
        m, c_all = membrane_step.shape[0], cavity_forward.shape[0]
        if m % nb == 0 and nb % nz == 0 and states.shape[1] == 8 and c_all == 8 * nb:
            return fast_body(nz, nb, states, membrane_step, cavity_forward, *rest)
        return plain_body(states, membrane_step, cavity_forward, *rest)

    return jax.shard_map(body, mesh=mesh, in_specs=in_specs, out_specs=out_specs, check_vma=False)
```

```python
import functools

import jax
import jax.numpy as jnp
from jax import lax
from jax.experimental import pallas as pl
from jax.experimental.pallas import tpu as pltpu
from jax.sharding import PartitionSpec as P

LANES = 128
GROUP_BLOCKS = 16
VMEM_LIMIT = 60 * 1024 * 1024


def plain_body(
    states, membrane_step, cavity_forward, coupling, membrane_forward, cavity_back, membrane_back
):
    highest = lax.Precision.HIGHEST
    panel_size, level_count, joint = states.shape
    levels_all = cavity_forward.shape[0]
    membrane_levels = membrane_step.shape[0]
    basis_total = float(levels_all * joint)
    head = jnp.einsum(
        "ab,scbr->scar",
        membrane_step,
        states.reshape(panel_size, level_count, membrane_levels, joint // membrane_levels),
        precision=highest,
    )
    head = head.reshape(panel_size, level_count, joint)
    panel_block = lax.all_to_all(head, "basis", split_axis=2, concat_axis=1, tiled=True)
    items, cavity_all, columns = panel_block.shape
    grid = jnp.einsum("qc,kcr->kqr", cavity_forward, panel_block, precision=highest)
    grid = jnp.einsum(
        "kqtm,nm->kqtn",
        grid.reshape(items, cavity_all, columns // membrane_levels, membrane_levels),
        membrane_forward,
        precision=highest,
    )
    weighted = grid * coupling[None, :, None, :]
    backward = jnp.einsum("kqtn,mn->kqtm", weighted, membrane_back, precision=highest)
    backward = backward.reshape(items, cavity_all, columns)
    stepped = jnp.einsum("cq,kqr->kcr", cavity_back, backward, precision=highest)
    spread = lax.all_to_all(stepped, "state", split_axis=2, concat_axis=0, tiled=True)
    state_total, spread_levels, spread_cols = spread.shape
    flattened = spread.reshape(state_total, -1)
    partial_gram = jnp.dot(flattened, flattened.T, precision=highest)
    gram = lax.psum(partial_gram, ("state", "basis")) / basis_total
    lower_factor = jnp.linalg.cholesky(gram)
    identity = jnp.eye(state_total, dtype=gram.dtype)
    inverse = lax.linalg.triangular_solve(lower_factor, identity, left_side=True, lower=True)
    local_result = jnp.dot(inverse, flattened, precision=highest)
    local_result = local_result.reshape(state_total, spread_levels, spread_cols)
    return lax.all_to_all(
        lax.all_to_all(local_result, "state", split_axis=0, concat_axis=2, tiled=True),
        "basis",
        split_axis=1,
        concat_axis=2,
        tiled=True,
    )


def split2(x):
    hi = x.astype(jnp.bfloat16)
    lo = (x - hi.astype(jnp.float32)).astype(jnp.bfloat16)
    return hi, lo


def bdot(a, b):
    return jnp.dot(a, b, preferred_element_type=jnp.float32)


def left3(wh, wl, x):
    xh, xl = split2(x)
    return bdot(jnp.concatenate([wh, wl, wh], axis=1), jnp.concatenate([xh, xh, xl], axis=0))


def right3(x, wh, wl):
    xh, xl = split2(x)
    return bdot(xh, wh) + bdot(xl, wh) + bdot(xh, wl)


def kron_left(w, reps, out_ref_h, out_ref_l):
    m = w.shape[0]
    n = m * reps
    row = lax.broadcasted_iota(jnp.int32, (n, m), 0)
    col = lax.broadcasted_iota(jnp.int32, (n, m), 1)
    left = (row // reps == col).astype(jnp.bfloat16)
    right_row = lax.broadcasted_iota(jnp.int32, (m, n), 0)
    right_col = lax.broadcasted_iota(jnp.int32, (m, n), 1)
    right = (right_col // reps == right_row).astype(jnp.bfloat16)
    a = lax.broadcasted_iota(jnp.int32, (n, n), 0)
    b = lax.broadcasted_iota(jnp.int32, (n, n), 1)
    keep = lax.rem(a, reps) == lax.rem(b, reps)
    for part, ref in zip(split2(w), (out_ref_h, out_ref_l)):
        full = bdot(bdot(left, part).astype(jnp.bfloat16), right)
        ref[...] = jnp.where(keep, full, 0.0).astype(jnp.bfloat16)


def kron_lanes(w_t, reps, out_ref_h, out_ref_l):
    m = w_t.shape[0]
    n = m * reps
    left = (
        lax.rem(lax.broadcasted_iota(jnp.int32, (n, m), 0), m)
        == lax.broadcasted_iota(jnp.int32, (n, m), 1)
    ).astype(jnp.bfloat16)
    right = (
        lax.rem(lax.broadcasted_iota(jnp.int32, (m, n), 1), m)
        == lax.broadcasted_iota(jnp.int32, (m, n), 0)
    ).astype(jnp.bfloat16)
    a = lax.broadcasted_iota(jnp.int32, (n, n), 0)
    b = lax.broadcasted_iota(jnp.int32, (n, n), 1)
    keep = a // m == b // m
    for part, ref in zip(split2(w_t), (out_ref_h, out_ref_l)):
        full = bdot(bdot(left, part).astype(jnp.bfloat16), right)
        ref[...] = jnp.where(keep, full, 0.0).astype(jnp.bfloat16)


def head_kernel(x_ref, w_ref, o_ref, kh, kl, xs):
    nb, nq, _, lev, width = o_ref.shape
    m = w_ref.shape[0]
    cols = x_ref.shape[2] // m

    @pl.when(pl.program_id(0) == 0)
    def _():
        kron_left(w_ref[...], lev, kh, kl)
        xs[...] = jnp.zeros_like(xs)

    for i in range(m):
        xs[i * lev : (i + 1) * lev, :cols] = x_ref[0, :, i * cols : (i + 1) * cols]
    xh, xl = split2(xs[...])
    y = bdot(kh[...], xh) + bdot(kl[...], xh) + bdot(kh[...], xl)
    o_ref[...] = y.reshape(nb, nq, 1, lev, width)


def remote(src, dst, send_sem, recv_sem, axis, peer):
    return pltpu.make_async_remote_copy(
        src_ref=src,
        dst_ref=dst,
        send_sem=send_sem,
        recv_sem=recv_sem,
        device_id={axis: peer},
        device_id_type=pl.DeviceIdType.MESH,
    )


def peers_of(axis, size):
    me = lax.axis_index(axis)
    return me, [lax.rem(me + d, size) for d in range(1, size)]


def state_peers(size):
    me = lax.axis_index("state")
    if size != 4:
        return peers_of("state", size)
    near = 3 - 2 * lax.rem(me, 2)
    return me, [lax.rem(me + d, size) for d in (2, near, 4 - near)]


def greet(nz, nb):
    barrier = pltpu.get_barrier_semaphore()
    for axis, size in (("basis", nb), ("state", nz)):
        for peer in peers_of(axis, size)[1]:
            pl.semaphore_signal(
                barrier, inc=1, device_id={axis: peer}, device_id_type=pl.DeviceIdType.MESH
            )
    pl.semaphore_wait(barrier, nb + nz - 2)


def gram_tiles(x_ref, q, accs, pairs):
    nz, half, ns, lev, width = x_ref.shape[1:]
    accs = list(accs)
    for h in range(half):
        for t in range(width // LANES):
            at = slice(t * LANES, (t + 1) * LANES)
            vals = [x_ref[q, a // ns, h, a % ns, :, at] for a in range(nz * ns)]
            for p, (a, b) in enumerate(pairs):
                accs[p] = accs[p] + vals[a] * vals[b]
    return tuple(accs)


def forward_kernel(
    nz,
    nb,
    x_ref,
    fc_ref,
    cp_ref,
    fk_ref,
    bc_ref,
    bk_ref,
    spread,
    gram_ref,
    fh,
    fl,
    bh,
    bl,
    cps,
    work,
    block,
    stepped,
    gram_b,
    gram_z,
    b_send,
    b_recv,
    z_send,
    z_recv,
    gb_send,
    gb_recv,
    gz_send,
    gz_recv,
):
    _, nq, ns, lev, width = x_ref.shape
    half = nb // nz
    total = nz * ns
    c_all = fc_ref.shape[0]
    m = fk_ref.shape[0]
    group = m * GROUP_BLOCKS
    me_b, others_b = peers_of("basis", nb)
    me_z, others_z = state_peers(nz)

    def to_basis(q, peer):
        return remote(
            x_ref.at[peer, q],
            block.at[q, me_b],
            b_send.at[q, peer],
            b_recv.at[q, me_b],
            "basis",
            peer,
        )

    def from_basis(q, peer):
        return remote(
            x_ref.at[me_b, q],
            block.at[q, peer],
            b_send.at[q, peer],
            b_recv.at[q, peer],
            "basis",
            peer,
        )

    def to_state(q, peer):
        return remote(
            stepped.at[q, peer],
            spread.at[q, me_z],
            z_send.at[q, peer],
            z_recv.at[q, me_z],
            "state",
            peer,
        )

    def from_state(q, peer):
        return remote(
            stepped.at[q, me_z],
            spread.at[q, peer],
            z_send.at[q, peer],
            z_recv.at[q, peer],
            "state",
            peer,
        )

    greet(nz, nb)

    @pl.loop(0, nq)
    def _(q):
        for peer in others_b:
            to_basis(q, peer).start()

    kron_lanes(fk_ref[...].T, GROUP_BLOCKS, fh, fl)
    kron_lanes(bk_ref[...].T, GROUP_BLOCKS, bh, bl)
    tile_m = (
        lax.rem(lax.broadcasted_iota(jnp.int32, (m, group), 1), m)
        == lax.broadcasted_iota(jnp.int32, (m, group), 0)
    ).astype(jnp.float32)
    cps[...] = jnp.dot(cp_ref[...], tile_m, precision=lax.Precision.HIGHEST)
    ch, cl = split2(fc_ref[...])
    dh, dl = split2(bc_ref[...])

    @pl.loop(0, nq)
    def _(q):
        block[q, me_b] = x_ref[me_b, q]
        for peer in others_b:
            from_basis(q, peer).wait_recv()
        for s in range(ns):
            x = block[q, :, s].reshape(c_all, width)
            work[s * c_all : (s + 1) * c_all, :] = left3(ch, cl, x)
        for at in range(0, width, group):
            n = min(group, width - at)
            g = right3(work[:, at : at + n], fh[:n, :n], fl[:n, :n])
            g = (g.reshape(ns, c_all, n) * cps[:, :n][None]).reshape(ns * c_all, n)
            work[:, at : at + n] = right3(g, bh[:n, :n], bl[:n, :n])
        for s in range(ns):
            y = left3(dh, dl, work[s * c_all : (s + 1) * c_all, :])
            stepped[q, :, :, s] = y.reshape(nz, half, lev, width)
        for peer in others_z:
            to_state(q, peer).start()
        spread[q, me_z] = stepped[q, me_z]

    pairs = [(a, b) for a in range(total) for b in range(a + 1)]

    def gram_chunk(q, accs):
        for peer in others_z:
            from_state(q, peer).wait_recv()
        return gram_tiles(spread, q, accs, pairs)

    zero = jnp.zeros((lev, LANES), jnp.float32)
    accs = lax.fori_loop(0, nq, gram_chunk, (zero,) * len(pairs))
    row = lax.broadcasted_iota(jnp.int32, (total, LANES), 0)
    col = lax.broadcasted_iota(jnp.int32, (total, LANES), 1)
    partial = jnp.zeros((total, LANES), jnp.float32)
    for p, (a, b) in enumerate(pairs):
        v = jnp.sum(jnp.sum(accs[p], axis=0, keepdims=True), axis=1, keepdims=True)
        here = ((row == a) & (col == b)) | ((row == b) & (col == a))
        partial = jnp.where(here, v, partial)

    def share(slots, send, recv, axis, me, others, value):
        slots[me] = value
        for peer in others:
            remote(slots.at[me], slots.at[me], send.at[peer], recv.at[me], axis, peer).start()
        for peer in others:
            remote(slots.at[me], slots.at[peer], send.at[peer], recv.at[peer], axis, peer).wait()
        out = slots[0]
        for i in range(1, slots.shape[0]):
            out = out + slots[i]
        return out

    partial = share(gram_b, gb_send, gb_recv, "basis", me_b, others_b, partial)
    gram_ref[...] = share(gram_z, gz_send, gz_recv, "state", me_z, others_z, partial)

    @pl.loop(0, nq)
    def _(q):
        for peer in others_b:
            to_basis(q, peer).wait_send()
        for peer in others_z:
            to_state(q, peer).wait_send()


def back_kernel(
    nz, nb, inv_ref, x_ref, o_ref, mixed, held, b_send, b_recv, z_send, z_recv
):
    nq, _, half, ns, lev, width = x_ref.shape
    total = nz * ns
    me_b, others_b = peers_of("basis", nb)
    me_z, others_z = state_peers(nz)

    def to_state(q, peer):
        return remote(
            mixed.at[q, peer],
            held.at[q, me_z],
            z_send.at[q, peer],
            z_recv.at[q, me_z],
            "state",
            peer,
        )

    def from_state(q, peer):
        return remote(
            mixed.at[q, me_z],
            held.at[q, peer],
            z_send.at[q, peer],
            z_recv.at[q, peer],
            "state",
            peer,
        )

    def to_basis(q, source, h):
        peer = source * half + h
        return remote(
            held.at[q, source, h],
            o_ref.at[q, me_b],
            b_send.at[q, peer],
            b_recv.at[q, me_b],
            "basis",
            peer,
        )

    def from_basis(q, peer):
        return remote(
            held.at[q, 0, 0],
            o_ref.at[q, peer],
            b_send.at[q, peer],
            b_recv.at[q, peer],
            "basis",
            peer,
        )

    greet(nz, nb)

    @pl.loop(0, nq)
    def _(q):
        for h in range(half):
            for t in range(width // LANES):
                at = slice(t * LANES, (t + 1) * LANES)
                vals = [x_ref[q, a // ns, h, a % ns, :, at] for a in range(total)]
                for b in range(total):
                    acc = inv_ref[b, 0] * vals[0]
                    for a in range(1, total):
                        acc = acc + inv_ref[b, a] * vals[a]
                    mixed[q, b // ns, h, b % ns, :, at] = acc
        for peer in others_z:
            to_state(q, peer).start()
        held[q, me_z] = mixed[q, me_z]

    def hand_on(q, source):
        for h in range(half):
            mine = source * half + h == me_b

            @pl.when(jnp.logical_not(mine))
            def _():
                to_basis(q, source, h).start()

            @pl.when(mine)
            def _():
                o_ref[q, me_b] = held[q, source, h]

    @pl.loop(0, nq)
    def _(q):
        hand_on(q, me_z)

    @pl.loop(0, nq)
    def _(q):
        for peer in others_z:
            from_state(q, peer).wait_recv()
            hand_on(q, peer)

    @pl.loop(0, nq)
    def _(q):
        for peer in others_b:
            from_basis(q, peer).wait_recv()
            from_basis(q, peer).wait_send()
        for peer in others_z:
            to_state(q, peer).wait_send()


def place_kernel(x_ref, o_ref):
    nq, nb, _, lev, width = x_ref.shape
    cols = o_ref.shape[2] // (nb * nq)
    for b in range(nb):
        for q in range(nq):
            i = b * nq + q
            o_ref[0, :, i * cols : (i + 1) * cols] = x_ref[q, b, 0, :, :cols]


def fast_body(
    nz,
    nb,
    states,
    membrane_step,
    cavity_forward,
    coupling,
    membrane_forward,
    cavity_back,
    membrane_back,
):
    f32 = jnp.float32
    ns, lev, joint = states.shape
    m = membrane_step.shape[0]
    c_all = cavity_forward.shape[0]
    nq, half = m // nb, nb // nz
    cols = joint // m
    width = -(-cols // LANES) * LANES
    group = m * GROUP_BLOCKS
    total = nz * ns
    dma = pltpu.SemaphoreType.DMA
    vmem = pl.BlockSpec(memory_space=pltpu.VMEM)
    params = pltpu.CompilerParams(vmem_limit_bytes=VMEM_LIMIT)
    whole = lambda a: pl.BlockSpec(a.shape, lambda *_: (0,) * a.ndim)

    head = pl.pallas_call(
        head_kernel,
        grid=(ns,),
        in_specs=[pl.BlockSpec((1, lev, joint), lambda s: (s, 0, 0)), whole(membrane_step)],
        out_specs=pl.BlockSpec((nb, nq, 1, lev, width), lambda s: (0, 0, s, 0, 0)),
        out_shape=jax.ShapeDtypeStruct((nb, nq, ns, lev, width), f32),
        scratch_shapes=[
            pltpu.VMEM((m * lev, m * lev), jnp.bfloat16),
            pltpu.VMEM((m * lev, m * lev), jnp.bfloat16),
            pltpu.VMEM((m * lev, width), f32),
        ],
        compiler_params=params,
    )(states, membrane_step)
    panel = (nq, nz, half, ns, lev, width)
    spread, gram = pl.pallas_call(
        functools.partial(forward_kernel, nz, nb),
        in_specs=[vmem] * 6,
        out_specs=[vmem, vmem],
        out_shape=[
            jax.ShapeDtypeStruct(panel, f32),
            jax.ShapeDtypeStruct((total, LANES), f32),
        ],
        scratch_shapes=[pltpu.VMEM((group, group), jnp.bfloat16)] * 4
        + [
            pltpu.VMEM((c_all, group), f32),
            pltpu.VMEM((ns * c_all, width), f32),
            pltpu.VMEM((nq, nb, ns, lev, width), f32),
            pltpu.VMEM(panel, f32),
            pltpu.VMEM((nb, total, LANES), f32),
            pltpu.VMEM((nz, total, LANES), f32),
        ]
        + [dma((nq, nb))] * 2
        + [dma((nq, nz))] * 2
        + [dma((nb,))] * 2
        + [dma((nz,))] * 2,
        compiler_params=pltpu.CompilerParams(
            vmem_limit_bytes=VMEM_LIMIT, collective_id=0, has_side_effects=True
        ),
    )(head, cavity_forward, coupling, membrane_forward, cavity_back, membrane_back)
    gram = gram[:, :total] / float(c_all * joint)
    lower_factor = jnp.linalg.cholesky(gram)
    identity = jnp.eye(total, dtype=f32)
    inverse = lax.linalg.triangular_solve(lower_factor, identity, left_side=True, lower=True)
    back = pl.pallas_call(
        functools.partial(back_kernel, nz, nb),
        in_specs=[pl.BlockSpec(memory_space=pltpu.SMEM), vmem],
        out_specs=vmem,
        out_shape=jax.ShapeDtypeStruct((nq, nb, ns, lev, width), f32),
        scratch_shapes=[pltpu.VMEM(panel, f32)] * 2
        + [dma((nq, nb))] * 2
        + [dma((nq, nz))] * 2,
        compiler_params=pltpu.CompilerParams(
            vmem_limit_bytes=VMEM_LIMIT, collective_id=1, has_side_effects=True
        ),
    )(inverse, spread)
    return pl.pallas_call(
        place_kernel,
        grid=(ns,),
        in_specs=[pl.BlockSpec((nq, nb, 1, lev, width), lambda s: (0, 0, s, 0, 0))],
        out_specs=pl.BlockSpec((1, lev, joint), lambda s: (s, 0, 0)),
        out_shape=jax.ShapeDtypeStruct((ns, lev, joint), f32),
        compiler_params=params,
    )(back)


def solution(mesh):
    nz, nb = mesh.shape["state"], mesh.shape["basis"]
    in_specs = (P("state", "basis", None), P(), P(), P(), P(), P(), P())
    out_specs = P("state", "basis", None)

    def body(states, membrane_step, cavity_forward, *rest):
        m, c_all = membrane_step.shape[0], cavity_forward.shape[0]
        if m % nb == 0 and nb % nz == 0 and states.shape[1] == 8 and c_all == 8 * nb:
            return fast_body(nz, nb, states, membrane_step, cavity_forward, *rest)
        return plain_body(states, membrane_step, cavity_forward, *rest)

    return jax.shard_map(body, mesh=mesh, in_specs=in_specs, out_specs=out_specs, check_vma=False)
```

```python
import functools

import jax
import jax.numpy as jnp
from jax import lax
from jax.experimental import pallas as pl
from jax.experimental.pallas import tpu as pltpu
from jax.sharding import PartitionSpec as P

LANES = 128
GROUP_BLOCKS = 16
VMEM_LIMIT = 60 * 1024 * 1024


def plain_body(
    states, membrane_step, cavity_forward, coupling, membrane_forward, cavity_back, membrane_back
):
    highest = lax.Precision.HIGHEST
    panel_size, level_count, joint = states.shape
    levels_all = cavity_forward.shape[0]
    membrane_levels = membrane_step.shape[0]
    basis_total = float(levels_all * joint)
    head = jnp.einsum(
        "ab,scbr->scar",
        membrane_step,
        states.reshape(panel_size, level_count, membrane_levels, joint // membrane_levels),
        precision=highest,
    )
    head = head.reshape(panel_size, level_count, joint)
    panel_block = lax.all_to_all(head, "basis", split_axis=2, concat_axis=1, tiled=True)
    items, cavity_all, columns = panel_block.shape
    grid = jnp.einsum("qc,kcr->kqr", cavity_forward, panel_block, precision=highest)
    grid = jnp.einsum(
        "kqtm,nm->kqtn",
        grid.reshape(items, cavity_all, columns // membrane_levels, membrane_levels),
        membrane_forward,
        precision=highest,
    )
    weighted = grid * coupling[None, :, None, :]
    backward = jnp.einsum("kqtn,mn->kqtm", weighted, membrane_back, precision=highest)
    backward = backward.reshape(items, cavity_all, columns)
    stepped = jnp.einsum("cq,kqr->kcr", cavity_back, backward, precision=highest)
    spread = lax.all_to_all(stepped, "state", split_axis=2, concat_axis=0, tiled=True)
    state_total, spread_levels, spread_cols = spread.shape
    flattened = spread.reshape(state_total, -1)
    partial_gram = jnp.dot(flattened, flattened.T, precision=highest)
    gram = lax.psum(partial_gram, ("state", "basis")) / basis_total
    lower_factor = jnp.linalg.cholesky(gram)
    identity = jnp.eye(state_total, dtype=gram.dtype)
    inverse = lax.linalg.triangular_solve(lower_factor, identity, left_side=True, lower=True)
    local_result = jnp.dot(inverse, flattened, precision=highest)
    local_result = local_result.reshape(state_total, spread_levels, spread_cols)
    return lax.all_to_all(
        lax.all_to_all(local_result, "state", split_axis=0, concat_axis=2, tiled=True),
        "basis",
        split_axis=1,
        concat_axis=2,
        tiled=True,
    )


def split2(x):
    hi = x.astype(jnp.bfloat16)
    lo = (x - hi.astype(jnp.float32)).astype(jnp.bfloat16)
    return hi, lo


def bdot(a, b):
    return jnp.dot(a, b, preferred_element_type=jnp.float32)


def left3(wh, wl, x):
    xh, xl = split2(x)
    return bdot(jnp.concatenate([wh, wl, wh], axis=1), jnp.concatenate([xh, xh, xl], axis=0))


def right3(x, wh, wl):
    xh, xl = split2(x)
    return bdot(xh, wh) + bdot(xl, wh) + bdot(xh, wl)


def kron_left(w, reps, out_ref_h, out_ref_l):
    m = w.shape[0]
    n = m * reps
    row = lax.broadcasted_iota(jnp.int32, (n, m), 0)
    col = lax.broadcasted_iota(jnp.int32, (n, m), 1)
    left = (row // reps == col).astype(jnp.bfloat16)
    right_row = lax.broadcasted_iota(jnp.int32, (m, n), 0)
    right_col = lax.broadcasted_iota(jnp.int32, (m, n), 1)
    right = (right_col // reps == right_row).astype(jnp.bfloat16)
    a = lax.broadcasted_iota(jnp.int32, (n, n), 0)
    b = lax.broadcasted_iota(jnp.int32, (n, n), 1)
    keep = lax.rem(a, reps) == lax.rem(b, reps)
    for part, ref in zip(split2(w), (out_ref_h, out_ref_l)):
        full = bdot(bdot(left, part).astype(jnp.bfloat16), right)
        ref[...] = jnp.where(keep, full, 0.0).astype(jnp.bfloat16)


def kron_lanes(w_t, reps, out_ref_h, out_ref_l):
    m = w_t.shape[0]
    n = m * reps
    left = (
        lax.rem(lax.broadcasted_iota(jnp.int32, (n, m), 0), m)
        == lax.broadcasted_iota(jnp.int32, (n, m), 1)
    ).astype(jnp.bfloat16)
    right = (
        lax.rem(lax.broadcasted_iota(jnp.int32, (m, n), 1), m)
        == lax.broadcasted_iota(jnp.int32, (m, n), 0)
    ).astype(jnp.bfloat16)
    a = lax.broadcasted_iota(jnp.int32, (n, n), 0)
    b = lax.broadcasted_iota(jnp.int32, (n, n), 1)
    keep = a // m == b // m
    for part, ref in zip(split2(w_t), (out_ref_h, out_ref_l)):
        full = bdot(bdot(left, part).astype(jnp.bfloat16), right)
        ref[...] = jnp.where(keep, full, 0.0).astype(jnp.bfloat16)


def remote(src, dst, send_sem, recv_sem, axis, peer):
    return pltpu.make_async_remote_copy(
        src_ref=src,
        dst_ref=dst,
        send_sem=send_sem,
        recv_sem=recv_sem,
        device_id={axis: peer},
        device_id_type=pl.DeviceIdType.MESH,
    )


def peers_of(axis, size):
    me = lax.axis_index(axis)
    return me, [lax.rem(me + d, size) for d in range(1, size)]


def state_peers(size):
    me = lax.axis_index("state")
    if size != 4:
        return peers_of("state", size)
    near = 3 - 2 * lax.rem(me, 2)
    return me, [lax.rem(me + d, size) for d in (2, near, 4 - near)]


def bulk_tiles(x_ref, q, h, low, nz, ns):
    width = x_ref.shape[-1]
    bulk = (width - LANES) // ns
    for t in range(bulk // LANES):
        yield t, [
            x_ref[q, a // ns, h, :, (a % ns) * bulk + t * LANES : (a % ns) * bulk + (t + 1) * LANES]
            for a in range(nz * ns)
        ]
    vals = []
    for z in range(nz):
        v = x_ref[q, z, h, :, width - LANES :]
        vals += [jnp.where(low, v, 0.0), jnp.where(low, pltpu.roll(v, LANES // 2, 1), 0.0)]
    yield None, vals


def step_kernel(
    nz,
    nb,
    x_ref,
    ms_ref,
    fc_ref,
    cp_ref,
    fk_ref,
    bc_ref,
    bk_ref,
    o_ref,
    xin,
    kh,
    kl,
    xs,
    outgo,
    fh,
    fl,
    bh,
    bl,
    cps,
    work,
    block,
    stepped,
    spread,
    gram_b,
    gram_z,
    splat,
    mixed,
    held,
    in_sem,
    b_send,
    b_recv,
    z_send,
    z_recv,
    gb_send,
    gb_recv,
    gz_send,
    gz_recv,
    y_send,
    y_recv,
    c_send,
    c_recv,
):
    _, nq, ns, lev, width = outgo.shape
    half = nb // nz
    total = nz * ns
    c_all = fc_ref.shape[0]
    m = fk_ref.shape[0]
    cols = x_ref.shape[2] // m
    group = m * GROUP_BLOCKS
    packed = ns * cols
    bulk = (packed - LANES) // ns
    pieces = [pl.ds(0, bulk), pl.ds(bulk, packed - bulk)]
    me_b, others_b = peers_of("basis", nb)
    me_z, others_z = state_peers(nz)
    low = lax.broadcasted_iota(jnp.int32, (lev, LANES), 1) < LANES // 2

    def to_basis(q, s, peer):
        return remote(
            outgo.at[peer, q, s],
            block.at[q, s, me_b],
            b_send.at[q, s, peer],
            b_recv.at[q, s, me_b],
            "basis",
            peer,
        )

    def from_basis(q, s, peer):
        return remote(
            outgo.at[me_b, q, s],
            block.at[q, s, peer],
            b_send.at[q, s, peer],
            b_recv.at[q, s, peer],
            "basis",
            peer,
        )

    def state_out(src, dst, send, recv, q, p, peer):
        return remote(
            src.at[q, peer, :, :, pieces[p]],
            dst.at[q, me_z, :, :, pieces[p]],
            send.at[q, p, peer],
            recv.at[q, p, me_z],
            "state",
            peer,
        )

    def state_in(src, dst, send, recv, q, p, peer):
        return remote(
            src.at[q, me_z, :, :, pieces[p]],
            dst.at[q, peer, :, :, pieces[p]],
            send.at[q, p, peer],
            recv.at[q, p, peer],
            "state",
            peer,
        )

    there = (stepped, spread, z_send, z_recv)
    again = (mixed, held, y_send, y_recv)

    def home_out(q, p, source, h):
        peer = source * half + h
        return remote(
            held.at[q, source, h, :, pieces[p]],
            o_ref.at[q, me_b, :, pieces[p]],
            c_send.at[q, p, peer],
            c_recv.at[q, p, me_b],
            "basis",
            peer,
        )

    def home_in(q, p, peer):
        return remote(
            held.at[q, 0, 0, :, pieces[p]],
            o_ref.at[q, peer, :, pieces[p]],
            c_send.at[q, p, peer],
            c_recv.at[q, p, peer],
            "basis",
            peer,
        )

    barrier = pltpu.get_barrier_semaphore()
    for axis, size in (("basis", nb), ("state", nz)):
        for peer in peers_of(axis, size)[1]:
            pl.semaphore_signal(
                barrier, inc=1, device_id={axis: peer}, device_id_type=pl.DeviceIdType.MESH
            )
    loads = [pltpu.make_async_copy(x_ref.at[s], xin.at[s], in_sem.at[s]) for s in range(ns)]
    for load in loads:
        load.start()
    kron_left(ms_ref[...], lev, kh, kl)
    xs[...] = jnp.zeros_like(xs)
    for s in range(ns):
        loads[s].wait()
        for i in range(m):
            xs[i * lev : (i + 1) * lev, :cols] = xin[s, :, i * cols : (i + 1) * cols]
        xh, xl = split2(xs[...])
        y = bdot(kh[...], xh) + bdot(kl[...], xh) + bdot(kh[...], xl)
        outgo[:, :, s] = y.reshape(nb, nq, lev, width)
        if s == 0:
            pl.semaphore_wait(barrier, nb + nz - 2)
        for peer in others_b:
            to_basis(0, s, peer).start()

    @pl.loop(1, nq)
    def _(q):
        for s in range(ns):
            for peer in others_b:
                to_basis(q, s, peer).start()

    kron_lanes(fk_ref[...].T, GROUP_BLOCKS, fh, fl)
    kron_lanes(bk_ref[...].T, GROUP_BLOCKS, bh, bl)
    tile_m = (
        lax.rem(lax.broadcasted_iota(jnp.int32, (m, group), 1), m)
        == lax.broadcasted_iota(jnp.int32, (m, group), 0)
    ).astype(jnp.float32)
    cps[...] = jnp.dot(cp_ref[...], tile_m, precision=lax.Precision.HIGHEST)
    ch, cl = split2(fc_ref[...])
    dh, dl = split2(bc_ref[...])

    @pl.loop(0, nq)
    def _(q):
        for s in range(ns):
            block[q, s, me_b] = outgo[me_b, q, s]
            for peer in others_b:
                from_basis(q, s, peer).wait_recv()
            work[...] = left3(ch, cl, block[q, s].reshape(c_all, width))
            for at in range(0, width, group):
                n = min(group, width - at)
                g = right3(work[:, at : at + n], fh[:n, :n], fl[:n, :n]) * cps[:, :n]
                work[:, at : at + n] = right3(g, bh[:n, :n], bl[:n, :n])
            y = left3(dh, dl, work[...])
            stepped[q, :, :, :, s * bulk : (s + 1) * bulk] = y[:, :bulk].reshape(
                nz, half, lev, bulk
            )
            tail = y[:, bulk:]
            if s == 0:
                first_tail = tail
            else:
                tail = jnp.where(
                    lax.broadcasted_iota(jnp.int32, tail.shape, 1) < LANES // 2,
                    first_tail,
                    pltpu.roll(tail, LANES // 2, 1),
                )
                stepped[q, :, :, :, packed - LANES :] = tail.reshape(nz, half, lev, LANES)
            for peer in others_z:
                state_out(*there, q, s, peer).start()
        spread[q, me_z] = stepped[q, me_z]

    pairs = [(a, b) for a in range(total) for b in range(a + 1)]

    def gram_chunk(q, accs):
        accs = list(accs)
        for p in range(ns):
            for peer in others_z:
                state_in(*there, q, p, peer).wait_recv()
        for h in range(half):
            for _, vals in bulk_tiles(spread, q, h, low, nz, ns):
                for p, (a, b) in enumerate(pairs):
                    accs[p] = accs[p] + vals[a] * vals[b]
        return tuple(accs)

    zero = jnp.zeros((lev, LANES), jnp.float32)
    accs = lax.fori_loop(0, nq, gram_chunk, (zero,) * len(pairs))
    row = lax.broadcasted_iota(jnp.int32, (total, LANES), 0)
    col = lax.broadcasted_iota(jnp.int32, (total, LANES), 1)
    partial = jnp.zeros((total, LANES), jnp.float32)
    for p, (a, b) in enumerate(pairs):
        v = jnp.sum(jnp.sum(accs[p], axis=0, keepdims=True), axis=1, keepdims=True)
        here = ((row == a) & (col == b)) | ((row == b) & (col == a))
        partial = jnp.where(here, v, partial)

    def share(slots, send, recv, axis, me, others, value):
        slots[me] = value
        for peer in others:
            remote(slots.at[me], slots.at[me], send.at[peer], recv.at[me], axis, peer).start()
        for peer in others:
            remote(slots.at[me], slots.at[peer], send.at[peer], recv.at[peer], axis, peer).wait()
        out = slots[0]
        for i in range(1, slots.shape[0]):
            out = out + slots[i]
        return out

    partial = share(gram_b, gb_send, gb_recv, "basis", me_b, others_b, partial)
    gram = share(gram_z, gz_send, gz_recv, "state", me_z, others_z, partial)
    gram = gram / float(c_all * m * cols)
    pair = jnp.where(col == row + total, 1.0, gram)
    diag = jnp.ones((total, 1), jnp.float32)
    for j in range(total):
        pivot = pair[j : j + 1, j : j + 1]
        diag = jnp.where(row[:, :1] == j, pivot, diag)
        if j < total - 1:
            factor = jnp.where(row[:, :1] > j, pair[:, j : j + 1] / pivot, 0.0)
            pair = pair - factor * pair[j : j + 1, :]
    pair = pair / jnp.sqrt(diag)
    for b in range(total):
        for a in range(total):
            splat[b * total + a] = jnp.broadcast_to(
                pair[b : b + 1, total + a : total + a + 1], (lev, LANES)
            )

    @pl.loop(0, nq)
    def _(q):
        for h in range(half):
            for t, vals in bulk_tiles(spread, q, h, low, nz, ns):
                for z in range(nz):
                    outs = []
                    for b in range(z * ns, (z + 1) * ns):
                        acc = splat[b * total] * vals[0]
                        for a in range(1, total):
                            acc = acc + splat[b * total + a] * vals[a]
                        outs.append(acc)
                    if t is None:
                        mixed[q, z, h, :, packed - LANES :] = jnp.where(
                            low, outs[0], pltpu.roll(outs[1], LANES // 2, 1)
                        )
                    else:
                        for s in range(ns):
                            at = s * bulk + t * LANES
                            mixed[q, z, h, :, at : at + LANES] = outs[s]
        for p in range(ns):
            for peer in others_z:
                state_out(*again, q, p, peer).start()
        held[q, me_z] = mixed[q, me_z]

    def hand_on(q, p, source):
        for h in range(half):
            mine = source * half + h == me_b

            @pl.when(jnp.logical_not(mine))
            def _():
                home_out(q, p, source, h).start()

            @pl.when(mine)
            def _():
                o_ref[q, me_b, :, pieces[p]] = held[q, source, h, :, pieces[p]]

    @pl.loop(0, nq)
    def _(q):
        for p in range(ns):
            hand_on(q, p, me_z)

    @pl.loop(0, nq)
    def _(q):
        for p in range(ns):
            for peer in others_z:
                state_in(*again, q, p, peer).wait_recv()
                hand_on(q, p, peer)

    @pl.loop(0, nq)
    def _(q):
        for p in range(ns):
            for peer in others_b:
                to_basis(q, p, peer).wait_send()
                home_in(q, p, peer).wait_recv()
                home_in(q, p, peer).wait_send()
            for peer in others_z:
                state_out(*there, q, p, peer).wait_send()
                state_out(*again, q, p, peer).wait_send()


def place_kernel(x_ref, o_ref):
    nq, here, lev, packed = x_ref.shape
    ns = o_ref.shape[0]
    cols = packed // ns
    bulk = (packed - LANES) // ns
    rest = cols - bulk
    for b in range(here):
        for q in range(nq):
            for s in range(ns):
                at = (b * nq + q) * cols
                tail = packed - LANES + s * rest
                o_ref[s, :, at : at + bulk] = x_ref[q, b, :, s * bulk : (s + 1) * bulk]
                o_ref[s, :, at + bulk : at + cols] = x_ref[q, b, :, tail : tail + rest]


def fast_body(
    nz,
    nb,
    states,
    membrane_step,
    cavity_forward,
    coupling,
    membrane_forward,
    cavity_back,
    membrane_back,
):
    f32, bf16 = jnp.float32, jnp.bfloat16
    ns, lev, joint = states.shape
    m = membrane_step.shape[0]
    c_all = cavity_forward.shape[0]
    nq, half = m // nb, nb // nz
    cols = joint // m
    width = -(-cols // LANES) * LANES
    group = m * GROUP_BLOCKS
    total = nz * ns
    dma = pltpu.SemaphoreType.DMA
    vmem = pl.BlockSpec(memory_space=pltpu.VMEM)
    panel = (nq, nz, half, lev, ns * cols)
    back = pl.pallas_call(
        functools.partial(step_kernel, nz, nb),
        in_specs=[pl.BlockSpec(memory_space=pl.ANY)] + [vmem] * 6,
        out_specs=vmem,
        out_shape=jax.ShapeDtypeStruct((nq, nb, lev, ns * cols), f32),
        scratch_shapes=[
            pltpu.VMEM((ns, lev, joint), f32),
            pltpu.VMEM((m * lev, m * lev), bf16),
            pltpu.VMEM((m * lev, m * lev), bf16),
            pltpu.VMEM((m * lev, width), f32),
            pltpu.VMEM((nb, nq, ns, lev, width), f32),
        ]
        + [pltpu.VMEM((group, group), bf16)] * 4
        + [
            pltpu.VMEM((c_all, group), f32),
            pltpu.VMEM((c_all, width), f32),
            pltpu.VMEM((nq, ns, nb, lev, width), f32),
            pltpu.VMEM(panel, f32),
            pltpu.VMEM(panel, f32),
            pltpu.VMEM((nb, total, LANES), f32),
            pltpu.VMEM((nz, total, LANES), f32),
            pltpu.VMEM((total * total, lev, LANES), f32),
            pltpu.VMEM(panel, f32),
            pltpu.VMEM(panel, f32),
            dma((ns,)),
        ]
        + [dma((nq, ns, nb))] * 2
        + [dma((nq, ns, nz))] * 2
        + [dma((nb,))] * 2
        + [dma((nz,))] * 2
        + [dma((nq, ns, nz))] * 2
        + [dma((nq, ns, nb))] * 2,
        compiler_params=pltpu.CompilerParams(
            vmem_limit_bytes=VMEM_LIMIT, collective_id=0, has_side_effects=True
        ),
    )(
        states,
        membrane_step,
        cavity_forward,
        coupling,
        membrane_forward,
        cavity_back,
        membrane_back,
    )
    return pl.pallas_call(
        place_kernel,
        grid=(nb // 2,),
        in_specs=[pl.BlockSpec((nq, 2, lev, ns * cols), lambda b: (0, b, 0, 0))],
        out_specs=pl.BlockSpec((ns, lev, 2 * nq * cols), lambda b: (0, 0, b)),
        out_shape=jax.ShapeDtypeStruct((ns, lev, joint), f32),
        compiler_params=pltpu.CompilerParams(vmem_limit_bytes=VMEM_LIMIT),
    )(back)


def solution(mesh):
    nz, nb = mesh.shape["state"], mesh.shape["basis"]
    in_specs = (P("state", "basis", None), P(), P(), P(), P(), P(), P())
    out_specs = P("state", "basis", None)

    def body(states, membrane_step, cavity_forward, *rest):
        m, c_all = membrane_step.shape[0], cavity_forward.shape[0]
        divides = m % nb == 0 and nb % nz == 0 and nb % 2 == 0
        packs = states.shape[0] == 2 and m * m % LANES == LANES // 2
        if divides and packs and states.shape[1] == 8 and c_all == 8 * nb:
            return fast_body(nz, nb, states, membrane_step, cavity_forward, *rest)
        return plain_body(states, membrane_step, cavity_forward, *rest)

    return jax.shard_map(body, mesh=mesh, in_specs=in_specs, out_specs=out_specs, check_vma=False)
```

```python
import functools

import jax
import jax.numpy as jnp
from jax import lax
from jax.experimental import pallas as pl
from jax.experimental.pallas import tpu as pltpu
from jax.sharding import PartitionSpec as P

LANES = 128
GROUP_BLOCKS = 16
VMEM_LIMIT = 60 * 1024 * 1024


def plain_body(
    states, membrane_step, cavity_forward, coupling, membrane_forward, cavity_back, membrane_back
):
    highest = lax.Precision.HIGHEST
    panel_size, level_count, joint = states.shape
    levels_all = cavity_forward.shape[0]
    membrane_levels = membrane_step.shape[0]
    basis_total = float(levels_all * joint)
    head = jnp.einsum(
        "ab,scbr->scar",
        membrane_step,
        states.reshape(panel_size, level_count, membrane_levels, joint // membrane_levels),
        precision=highest,
    )
    head = head.reshape(panel_size, level_count, joint)
    panel_block = lax.all_to_all(head, "basis", split_axis=2, concat_axis=1, tiled=True)
    items, cavity_all, columns = panel_block.shape
    grid = jnp.einsum("qc,kcr->kqr", cavity_forward, panel_block, precision=highest)
    grid = jnp.einsum(
        "kqtm,nm->kqtn",
        grid.reshape(items, cavity_all, columns // membrane_levels, membrane_levels),
        membrane_forward,
        precision=highest,
    )
    weighted = grid * coupling[None, :, None, :]
    backward = jnp.einsum("kqtn,mn->kqtm", weighted, membrane_back, precision=highest)
    backward = backward.reshape(items, cavity_all, columns)
    stepped = jnp.einsum("cq,kqr->kcr", cavity_back, backward, precision=highest)
    spread = lax.all_to_all(stepped, "state", split_axis=2, concat_axis=0, tiled=True)
    state_total, spread_levels, spread_cols = spread.shape
    flattened = spread.reshape(state_total, -1)
    partial_gram = jnp.dot(flattened, flattened.T, precision=highest)
    gram = lax.psum(partial_gram, ("state", "basis")) / basis_total
    lower_factor = jnp.linalg.cholesky(gram)
    identity = jnp.eye(state_total, dtype=gram.dtype)
    inverse = lax.linalg.triangular_solve(lower_factor, identity, left_side=True, lower=True)
    local_result = jnp.dot(inverse, flattened, precision=highest)
    local_result = local_result.reshape(state_total, spread_levels, spread_cols)
    return lax.all_to_all(
        lax.all_to_all(local_result, "state", split_axis=0, concat_axis=2, tiled=True),
        "basis",
        split_axis=1,
        concat_axis=2,
        tiled=True,
    )


def split2(x):
    hi = x.astype(jnp.bfloat16)
    lo = (x - hi.astype(jnp.float32)).astype(jnp.bfloat16)
    return hi, lo


def bdot(a, b):
    return jnp.dot(a, b, preferred_element_type=jnp.float32)


def left3(wh, wl, x):
    xh, xl = split2(x)
    return bdot(jnp.concatenate([wh, wl, wh], axis=1), jnp.concatenate([xh, xh, xl], axis=0))


def right3(x, wh, wl):
    xh, xl = split2(x)
    return bdot(xh, wh) + bdot(xl, wh) + bdot(xh, wl)


def kron_left(w, reps, out_ref_h, out_ref_l):
    m = w.shape[0]
    n = m * reps
    row = lax.broadcasted_iota(jnp.int32, (n, m), 0)
    col = lax.broadcasted_iota(jnp.int32, (n, m), 1)
    left = (row // reps == col).astype(jnp.bfloat16)
    right_row = lax.broadcasted_iota(jnp.int32, (m, n), 0)
    right_col = lax.broadcasted_iota(jnp.int32, (m, n), 1)
    right = (right_col // reps == right_row).astype(jnp.bfloat16)
    a = lax.broadcasted_iota(jnp.int32, (n, 1), 0)
    b = lax.broadcasted_iota(jnp.int32, (1, n), 1)
    keep = lax.rem(a, reps) == lax.rem(b, reps)
    for part, ref in zip(split2(w), (out_ref_h, out_ref_l)):
        full = bdot(bdot(left, part).astype(jnp.bfloat16), right)
        ref[...] = jnp.where(keep, full, 0.0).astype(jnp.bfloat16)


def kron_lanes(w_t, reps, out_ref_h, out_ref_l):
    m = w_t.shape[0]
    n = m * reps
    left = (
        lax.rem(lax.broadcasted_iota(jnp.int32, (n, m), 0), m)
        == lax.broadcasted_iota(jnp.int32, (n, m), 1)
    ).astype(jnp.bfloat16)
    right = (
        lax.rem(lax.broadcasted_iota(jnp.int32, (m, n), 1), m)
        == lax.broadcasted_iota(jnp.int32, (m, n), 0)
    ).astype(jnp.bfloat16)
    a = lax.broadcasted_iota(jnp.int32, (n, 1), 0)
    b = lax.broadcasted_iota(jnp.int32, (1, n), 1)
    keep = a // m == b // m
    for part, ref in zip(split2(w_t), (out_ref_h, out_ref_l)):
        full = bdot(bdot(left, part).astype(jnp.bfloat16), right)
        ref[...] = jnp.where(keep, full, 0.0).astype(jnp.bfloat16)


def remote(src, dst, send_sem, recv_sem, axis, peer):
    return pltpu.make_async_remote_copy(
        src_ref=src,
        dst_ref=dst,
        send_sem=send_sem,
        recv_sem=recv_sem,
        device_id={axis: peer},
        device_id_type=pl.DeviceIdType.MESH,
    )


def peers_of(axis, size):
    me = lax.axis_index(axis)
    return me, [lax.rem(me + d, size) for d in range(1, size)]


def state_peers(size):
    me = lax.axis_index("state")
    if size != 4:
        return peers_of("state", size)
    near = 3 - 2 * lax.rem(me, 2)
    return me, [lax.rem(me + d, size) for d in (2, near, 4 - near)]


def bulk_tiles(x_ref, q, h, low, nz, ns):
    width = x_ref.shape[-1]
    bulk = (width - LANES) // ns
    for t in range(bulk // LANES):
        yield t, [
            x_ref[q, a // ns, h, :, (a % ns) * bulk + t * LANES : (a % ns) * bulk + (t + 1) * LANES]
            for a in range(nz * ns)
        ]
    vals = []
    for z in range(nz):
        v = x_ref[q, z, h, :, width - LANES :]
        vals += [jnp.where(low, v, 0.0), jnp.where(low, pltpu.roll(v, LANES // 2, 1), 0.0)]
    yield None, vals


def step_kernel(
    nz,
    nb,
    x_ref,
    ms_ref,
    fc_ref,
    cp_ref,
    fk_ref,
    bc_ref,
    bk_ref,
    o_ref,
    xin,
    kh,
    kl,
    xs,
    outgo,
    fh,
    fl,
    bh,
    bl,
    cps,
    work,
    block,
    stepped,
    spread,
    gram_b,
    gram_z,
    splat,
    mixed,
    held,
    home,
    in_sem,
    b_send,
    b_recv,
    z_send,
    z_recv,
    gb_send,
    gb_recv,
    gz_send,
    gz_recv,
    y_send,
    y_recv,
    c_send,
    c_recv,
):
    _, nq, ns, lev, width = outgo.shape
    half = nb // nz
    total = nz * ns
    c_all = fc_ref.shape[0]
    m = fk_ref.shape[0]
    cols = x_ref.shape[2] // m
    group = m * GROUP_BLOCKS
    packed = ns * cols
    bulk = (packed - LANES) // ns
    pieces = [pl.ds(0, bulk), pl.ds(bulk, packed - bulk)]
    me_b, others_b = peers_of("basis", nb)
    me_z, others_z = state_peers(nz)
    low = lax.broadcasted_iota(jnp.int32, (lev, LANES), 1) < LANES // 2

    def to_basis(q, s, peer):
        return remote(
            outgo.at[peer, q, s],
            block.at[q, s, me_b],
            b_send.at[q, s, peer],
            b_recv.at[q, s, me_b],
            "basis",
            peer,
        )

    def from_basis(q, s, peer):
        return remote(
            outgo.at[me_b, q, s],
            block.at[q, s, peer],
            b_send.at[q, s, peer],
            b_recv.at[q, s, peer],
            "basis",
            peer,
        )

    def state_out(src, dst, send, recv, q, p, peer):
        return remote(
            src.at[q, peer, :, :, pieces[p]],
            dst.at[q, me_z, :, :, pieces[p]],
            send.at[q, p, peer],
            recv.at[q, p, me_z],
            "state",
            peer,
        )

    def state_in(src, dst, send, recv, q, p, peer):
        return remote(
            src.at[q, me_z, :, :, pieces[p]],
            dst.at[q, peer, :, :, pieces[p]],
            send.at[q, p, peer],
            recv.at[q, p, peer],
            "state",
            peer,
        )

    there = (stepped, spread, z_send, z_recv)
    again = (mixed, held, y_send, y_recv)

    def home_out(q, p, source, h):
        peer = source * half + h
        return remote(
            held.at[q, source, h, :, pieces[p]],
            home.at[q, me_b, :, pieces[p]],
            c_send.at[q, p, peer],
            c_recv.at[q, p, me_b],
            "basis",
            peer,
        )

    def home_in(q, p, peer):
        return remote(
            held.at[q, 0, 0, :, pieces[p]],
            home.at[q, peer, :, pieces[p]],
            c_send.at[q, p, peer],
            c_recv.at[q, p, peer],
            "basis",
            peer,
        )

    barrier = pltpu.get_barrier_semaphore()
    for axis, size in (("basis", nb), ("state", nz)):
        for peer in peers_of(axis, size)[1]:
            pl.semaphore_signal(
                barrier, inc=1, device_id={axis: peer}, device_id_type=pl.DeviceIdType.MESH
            )
    loads = [pltpu.make_async_copy(x_ref.at[s], xin.at[s], in_sem.at[s]) for s in range(ns)]
    for load in loads:
        load.start()
    kron_left(ms_ref[...], lev, kh, kl)
    xs[...] = jnp.zeros_like(xs)
    for s in range(ns):
        loads[s].wait()
        for i in range(m):
            xs[i * lev : (i + 1) * lev, :cols] = xin[s, :, i * cols : (i + 1) * cols]
        xh, xl = split2(xs[...])
        y = bdot(kh[...], xh) + bdot(kl[...], xh) + bdot(kh[...], xl)
        outgo[:, :, s] = y.reshape(nb, nq, lev, width)
        if s == 0:
            pl.semaphore_wait(barrier, nb + nz - 2)
        for peer in others_b:
            to_basis(0, s, peer).start()

    @pl.loop(1, nq)
    def _(q):
        for s in range(ns):
            for peer in others_b:
                to_basis(q, s, peer).start()

    kron_lanes(fk_ref[...].T, GROUP_BLOCKS, fh, fl)
    kron_lanes(bk_ref[...].T, GROUP_BLOCKS, bh, bl)
    tile_m = (
        lax.rem(lax.broadcasted_iota(jnp.int32, (m, group), 1), m)
        == lax.broadcasted_iota(jnp.int32, (m, group), 0)
    ).astype(jnp.float32)
    cps[...] = jnp.dot(cp_ref[...].T, tile_m, precision=lax.Precision.HIGHEST)
    ch, cl = split2(fc_ref[...])
    dh, dl = split2(bc_ref[...])

    @pl.loop(0, nq)
    def _(q):
        for s in range(ns):
            block[q, s, me_b] = outgo[me_b, q, s]
            for peer in others_b:
                from_basis(q, s, peer).wait_recv()
            work[...] = left3(ch, cl, block[q, s].reshape(c_all, width))
            for at in range(0, width, group):
                n = min(group, width - at)
                g = right3(work[:, at : at + n], fh[:n, :n], fl[:n, :n]) * cps[:, :n]
                work[:, at : at + n] = right3(g, bh[:n, :n], bl[:n, :n])
            y = left3(dh, dl, work[...])
            stepped[q, :, :, :, s * bulk : (s + 1) * bulk] = y[:, :bulk].reshape(
                nz, half, lev, bulk
            )
            tail = y[:, bulk:]
            if s == 0:
                first_tail = tail
            else:
                tail = jnp.where(
                    lax.broadcasted_iota(jnp.int32, tail.shape, 1) < LANES // 2,
                    first_tail,
                    pltpu.roll(tail, LANES // 2, 1),
                )
                stepped[q, :, :, :, packed - LANES :] = tail.reshape(nz, half, lev, LANES)
            for peer in others_z:
                state_out(*there, q, s, peer).start()
        spread[q, me_z] = stepped[q, me_z]

    pairs = [(a, b) for a in range(total) for b in range(a + 1)]

    def gram_chunk(q, accs):
        accs = list(accs)
        for p in range(ns):
            for peer in others_z:
                state_in(*there, q, p, peer).wait_recv()
        for h in range(half):
            for _, vals in bulk_tiles(spread, q, h, low, nz, ns):
                for p, (a, b) in enumerate(pairs):
                    accs[p] = accs[p] + vals[a] * vals[b]
        return tuple(accs)

    zero = jnp.zeros((lev, LANES), jnp.float32)
    accs = lax.fori_loop(0, nq, gram_chunk, (zero,) * len(pairs))
    row = lax.broadcasted_iota(jnp.int32, (total, LANES), 0)
    col = lax.broadcasted_iota(jnp.int32, (total, LANES), 1)
    partial = jnp.zeros((total, LANES), jnp.float32)
    for p, (a, b) in enumerate(pairs):
        v = jnp.sum(jnp.sum(accs[p], axis=0, keepdims=True), axis=1, keepdims=True)
        here = ((row == a) & (col == b)) | ((row == b) & (col == a))
        partial = jnp.where(here, v, partial)

    def share(slots, send, recv, axis, me, others, value):
        slots[me] = value
        for peer in others:
            remote(slots.at[me], slots.at[me], send.at[peer], recv.at[me], axis, peer).start()
        for peer in others:
            remote(slots.at[me], slots.at[peer], send.at[peer], recv.at[peer], axis, peer).wait()
        out = slots[0]
        for i in range(1, slots.shape[0]):
            out = out + slots[i]
        return out

    partial = share(gram_b, gb_send, gb_recv, "basis", me_b, others_b, partial)
    gram = share(gram_z, gz_send, gz_recv, "state", me_z, others_z, partial)
    gram = gram / float(c_all * m * cols)
    pair = jnp.where(col == row + total, 1.0, gram)
    diag = jnp.ones((total, 1), jnp.float32)
    for j in range(total):
        pivot = pair[j : j + 1, j : j + 1]
        diag = jnp.where(row[:, :1] == j, pivot, diag)
        if j < total - 1:
            factor = jnp.where(row[:, :1] > j, pair[:, j : j + 1] / pivot, 0.0)
            pair = pair - factor * pair[j : j + 1, :]
    pair = pair / jnp.sqrt(diag)
    for b in range(total):
        for a in range(total):
            splat[b * total + a] = jnp.broadcast_to(
                pair[b : b + 1, total + a : total + a + 1], (lev, LANES)
            )

    @pl.loop(0, nq)
    def _(q):
        for p in range(ns):
            for h in range(half):
                for t, vals in bulk_tiles(spread, q, h, low, nz, ns):
                    if t is None and p < ns - 1:
                        continue
                    for z in range(nz):
                        outs = []
                        for s in range(ns) if t is None else (p,):
                            b = z * ns + s
                            acc = splat[b * total] * vals[0]
                            for a in range(1, total):
                                acc = acc + splat[b * total + a] * vals[a]
                            outs.append(acc)
                        if t is None:
                            mixed[q, z, h, :, packed - LANES :] = jnp.where(
                                low, outs[0], pltpu.roll(outs[1], LANES // 2, 1)
                            )
                        else:
                            at = p * bulk + t * LANES
                            mixed[q, z, h, :, at : at + LANES] = outs[0]
            for peer in others_z:
                state_out(*again, q, p, peer).start()
        held[q, me_z] = mixed[q, me_z]

    def hand_on(q, p, source):
        for h in range(half):
            mine = source * half + h == me_b

            @pl.when(jnp.logical_not(mine))
            def _():
                home_out(q, p, source, h).start()

            @pl.when(mine)
            def _():
                home[q, me_b, :, pieces[p]] = held[q, source, h, :, pieces[p]]

    @pl.loop(0, nq)
    def _(q):
        for p in range(ns):
            hand_on(q, p, me_z)

    def place(q, p):
        for peer in others_b:
            home_in(q, p, peer).wait_recv()
        for b in range(nb):
            at = (b * nq + q) * cols
            o_ref[p, :, at : at + bulk] = home[q, b, :, p * bulk : (p + 1) * bulk]
            if p == ns - 1:
                for s in range(ns):
                    tail = packed - LANES + s * (cols - bulk)
                    o_ref[s, :, at + bulk : at + cols] = home[q, b, :, tail : tail + cols - bulk]

    order = [(q, p) for q in range(nq) for p in range(ns)]
    for k, (q, p) in enumerate(order):
        for peer in others_z:
            state_in(*again, q, p, peer).wait_recv()
            hand_on(q, p, peer)
        if k > 0:
            place(*order[k - 1])
    place(*order[-1])

    @pl.loop(0, nq)
    def _(q):
        for p in range(ns):
            for peer in others_b:
                to_basis(q, p, peer).wait_send()
                home_in(q, p, peer).wait_send()
            for peer in others_z:
                state_out(*there, q, p, peer).wait_send()
                state_out(*again, q, p, peer).wait_send()


def fast_body(
    nz,
    nb,
    states,
    membrane_step,
    cavity_forward,
    coupling,
    membrane_forward,
    cavity_back,
    membrane_back,
):
    f32, bf16 = jnp.float32, jnp.bfloat16
    ns, lev, joint = states.shape
    m = membrane_step.shape[0]
    c_all = cavity_forward.shape[0]
    nq, half = m // nb, nb // nz
    cols = joint // m
    width = -(-cols // LANES) * LANES
    group = m * GROUP_BLOCKS
    total = nz * ns
    dma = pltpu.SemaphoreType.DMA
    vmem = pl.BlockSpec(memory_space=pltpu.VMEM)
    panel = (nq, nz, half, lev, ns * cols)
    return pl.pallas_call(
        functools.partial(step_kernel, nz, nb),
        in_specs=[pl.BlockSpec(memory_space=pl.ANY)] + [vmem] * 6,
        out_specs=vmem,
        out_shape=jax.ShapeDtypeStruct((ns, lev, joint), f32),
        scratch_shapes=[
            pltpu.VMEM((ns, lev, joint), f32),
            pltpu.VMEM((m * lev, m * lev), bf16),
            pltpu.VMEM((m * lev, m * lev), bf16),
            pltpu.VMEM((m * lev, width), f32),
            pltpu.VMEM((nb, nq, ns, lev, width), f32),
        ]
        + [pltpu.VMEM((group, group), bf16)] * 4
        + [
            pltpu.VMEM((c_all, group), f32),
            pltpu.VMEM((c_all, width), f32),
            pltpu.VMEM((nq, ns, nb, lev, width), f32),
            pltpu.VMEM(panel, f32),
            pltpu.VMEM(panel, f32),
            pltpu.VMEM((nb, total, LANES), f32),
            pltpu.VMEM((nz, total, LANES), f32),
            pltpu.VMEM((total * total, lev, LANES), f32),
            pltpu.VMEM(panel, f32),
            pltpu.VMEM(panel, f32),
            pltpu.VMEM((nq, nb, lev, ns * cols), f32),
            dma((ns,)),
        ]
        + [dma((nq, ns, nb))] * 2
        + [dma((nq, ns, nz))] * 2
        + [dma((nb,))] * 2
        + [dma((nz,))] * 2
        + [dma((nq, ns, nz))] * 2
        + [dma((nq, ns, nb))] * 2,
        compiler_params=pltpu.CompilerParams(
            vmem_limit_bytes=VMEM_LIMIT, collective_id=0, has_side_effects=True
        ),
    )(
        states,
        membrane_step,
        cavity_forward,
        coupling.T,
        membrane_forward,
        cavity_back,
        membrane_back,
    )


def solution(mesh):
    nz, nb = mesh.shape["state"], mesh.shape["basis"]
    in_specs = (P("state", "basis", None), P(), P(), P(), P(), P(), P())
    out_specs = P("state", "basis", None)

    def body(states, membrane_step, cavity_forward, *rest):
        m, c_all = membrane_step.shape[0], cavity_forward.shape[0]
        divides = m % nb == 0 and nb % nz == 0 and nb % 2 == 0
        packs = states.shape[0] == 2 and m * m % LANES == LANES // 2
        if divides and packs and states.shape[1] == 8 and c_all == 8 * nb:
            return fast_body(nz, nb, states, membrane_step, cavity_forward, *rest)
        return plain_body(states, membrane_step, cavity_forward, *rest)

    return jax.shard_map(body, mesh=mesh, in_specs=in_specs, out_specs=out_specs, check_vma=False)
```
